128 devices in a mesh: row: 16 (over y, z_hi, core), col: 8 (over x, z_lo).
Axes of the slice: x: 4, y: 4, z: 4 (z_hi: 2, z_lo: 2; z = z_hi * 2 + z_lo), core: 2. Of those that a mesh axis runs over, the one named last changes fastest.
Arguments:
- embed: bfloat16 [32768, 512], P(('row', 'col')), may hold values from -6 to 6
- target: int32 [32768], P(('row', 'col')), may hold values from 0 to 32767, as said below
- weight: bfloat16 [512, 512], replicated, may hold values from -0.25 to 0.25
- bias: float32 [512], replicated, may hold values from -4 to 4
- block_row: int32 [16, 8, 128], P('row', 'col'), may hold values from 0 to 15, as said below
- block_col: int32 [16, 8, 128], P('row', 'col'), may hold values from 0 to 31
- block_live: int32 [16, 8], P('row', 'col'), may hold values from 32 to 128, as said below
- edge_count: int32 [16, 8, 128, 128, 128], P('row', 'col'), may hold values from 0 to 4
- upstream: bfloat16 [32768, 512], P('row'), may hold values from -6 to 6
Outputs:
- layer_out: bfloat16 [32768, 512], P(('row', 'col'))
- account_grad: bfloat16 [32768, 512], P(('col', 'row'))
The draws below stay inside these ranges and needn't reach their ends.
Inputs may be any that keep to these rules, and one draw needn't show every extreme that they name: `target`: a permutation of the accounts; account a belongs to grid shard a // 256; the 256 rows of one encoder device bound for one grid shard number at most 3, and every encoder device sends exactly 3 to some shard. Within one tile the 128 pairs (block_row, block_col) are distinct. `block_live`: some tile has all 128 slots nonempty.
All inputs are finite; a program needn't handle non-finite values.
Results may differ from the reference program's by a relative error of at most 0.013.
Values may be sent and summed in bfloat16 or wider, within the bound.
No kernel may reach another device: no remote copies, remote signals or barrier semaphores. Data moves between devices by JAX's collectives and lax.ppermute only.
A program may use at most 128 MiB of HBM per device.

```python
import jax
import jax.numpy as jnp
from jax import lax

F = 512
BS = 128
NODE_DEV = 256
CAP = 128
ROW_TILES = 16
COL_TILES = 8
NODES = 32768
ROWB = 16
COLB = 32


def block_layout(key):
    tile_count = ROW_TILES * COL_TILES
    spot_count = ROWB * COLB
    tile_keys = jax.random.split(jax.random.fold_in(key, 101), tile_count)
    chosen = jax.vmap(lambda k: jax.random.permutation(k, spot_count)[:CAP])(tile_keys).astype(jnp.int32)
    tile_rows = (chosen // COLB).reshape(ROW_TILES, COL_TILES, CAP)
    tile_cols = (chosen % COLB).reshape(ROW_TILES, COL_TILES, CAP)
    live_count = jax.random.randint(jax.random.fold_in(key, 102), (tile_count,), CAP // 4, CAP // 2 + 1)
    busiest = jax.random.randint(jax.random.fold_in(key, 103), (), 0, tile_count)
    live_count = jnp.where(jnp.arange(tile_count) == busiest, CAP, live_count).astype(jnp.int32)
    return (tile_rows, tile_cols, live_count.reshape(ROW_TILES, COL_TILES))


def draw_block_row(key, part):
    return block_layout(key)[0]


def draw_block_col(key, part):
    return block_layout(key)[1]


def draw_block_live(key, part):
    return block_layout(key)[2]


def draw_edge_count(key, part):
    tile_rows, tile_cols, live_count = block_layout(key)
    global_col = jnp.arange(COL_TILES, dtype=jnp.int32)[None, :, None] * COLB + tile_cols
    chance = 80 + 160 * global_col // (COLB * COL_TILES)
    global_row = jnp.arange(ROW_TILES, dtype=jnp.int32)[:, None, None] * ROWB + tile_rows
    active = jax.random.randint(jax.random.fold_in(key, 104), (NODES,), 0, 16) != 0
    row_nodes = global_row[..., None] * BS + jnp.arange(BS, dtype=jnp.int32)
    row_active = active[row_nodes]
    raw_draw = jax.random.randint(jax.random.fold_in(key, 105), (ROW_TILES, COL_TILES, CAP, BS, BS), 0, 4000)
    edge_value = 1 + raw_draw % 4
    kept = (raw_draw < chance[..., None, None]) & row_active[..., None]
    return jnp.where(kept, edge_value, 0).astype(jnp.int32)


def draw_target(key, part):
    tile_count = ROW_TILES * COL_TILES
    per_pair = NODE_DEV // tile_count
    steps_up = jax.random.randint(jax.random.fold_in(key, 201), (tile_count,), 0, per_pair)
    steps_up = steps_up.at[0].set(per_pair - 1).at[tile_count - 1].set(0)
    jumps = steps_up - jnp.roll(steps_up, 1)
    lag = (jnp.arange(tile_count)[None, :] - jnp.arange(tile_count)[:, None]) % tile_count
    pair_count = per_pair + jumps[lag]
    cum_count = jnp.cumsum(pair_count, axis=1)
    start_count = cum_count - pair_count
    dest_offset = jnp.cumsum(pair_count, axis=0) - pair_count
    positions = jnp.arange(NODE_DEV, dtype=jnp.int32)
    dest_shard = jax.vmap(lambda c: jnp.searchsorted(c, positions, side='right'))(cum_count).astype(jnp.int32)
    slot_in = jnp.take_along_axis(dest_offset, dest_shard, 1) + positions[None, :] - jnp.take_along_axis(start_count, dest_shard, 1)
    account = dest_shard * NODE_DEV + slot_in
    shuffle_keys = jax.random.split(jax.random.fold_in(key, 202), tile_count)
    shuffles = jax.vmap(lambda k: jax.random.permutation(k, NODE_DEV))(shuffle_keys)
    source_ids = jnp.arange(tile_count)[:, None]
    placed = jnp.zeros((tile_count, NODE_DEV), jnp.int32).at[source_ids, shuffles].set(account.astype(jnp.int32))
    return placed.reshape(NODES).astype(jnp.int32)


def level_of(own_key, shape, pieces, least, high):
    def one(dim, blocks):
        heights = jax.random.uniform(jax.random.fold_in(jax.random.fold_in(own_key, 6), dim), (blocks,), jnp.float32, least / len(pieces), high / len(pieces))
        return jnp.repeat(jnp.exp(heights), shape[dim] // blocks).reshape((-1,) + (1,) * (len(shape) - dim - 1))

    factor_of = one(*pieces[0])
    for cut in pieces[1:]:
        factor_of = factor_of * one(*cut)
    return factor_of


def scatter_about(key, dims, spread, most, shards=(), kind=jnp.bfloat16):
    array = jax.random.normal(key, dims, jnp.float32) * spread
    if len(shards) > 0:
        array = level_of(key, dims, shards, -0.22, 0.18) * array
    return jnp.clip(array, min=-most, max=most).astype(kind)


def setup_inputs(seed: int = 0) -> dict:
    keys = jax.random.split(jax.random.key(seed), 10)
    embed = scatter_about(keys[0], (NODES, F), 1.0, 6.0, ((0, 128),))
    target = draw_target(jax.random.fold_in(keys[9], 71), 0)
    weight = scatter_about(keys[2], (F, F), F ** -0.5, 0.25)
    bias = scatter_about(keys[3], (F,), 1.0, 4.0, (), jnp.float32)
    block_row = draw_block_row(jax.random.fold_in(keys[9], 71), 0)
    block_col = draw_block_col(jax.random.fold_in(keys[9], 71), 0)
    block_live = draw_block_live(jax.random.fold_in(keys[9], 71), 0)
    edge_count = draw_edge_count(jax.random.fold_in(keys[9], 71), 0)
    upstream = scatter_about(keys[8], (NODES, F), 1.0, 6.0, ((0, 16),))
    return dict(embed=embed, target=target, weight=weight, bias=bias, block_row=block_row, block_col=block_col, block_live=block_live, edge_count=edge_count, upstream=upstream)


def silu_slope(v):
    logistic = jax.nn.sigmoid(v)
    return logistic * (1.0 + v * (1.0 - logistic))

def reference(embed, target, weight, bias, block_row, block_col, block_live, edge_count, upstream):
    tile_count = ROW_TILES * COL_TILES
    blocks_all = NODES // BS
    features = jnp.zeros((NODES, F), jnp.bfloat16).at[target].set(embed)
    feat_blocks = features.reshape(blocks_all, BS, F)
    tile_rows = block_row.reshape(tile_count, CAP)
    tile_cols = block_col.reshape(tile_count, CAP)
    live_all = block_live.reshape(tile_count)
    counts_all = edge_count.reshape(tile_count, CAP, BS, BS)
    slot_ids = jnp.arange(CAP, dtype=jnp.int32)

    def tile_parts(t):
        tile_row = t // COL_TILES
        tile_col = t % COL_TILES
        global_row = tile_row * ROWB + tile_rows[t]
        global_col = tile_col * COLB + tile_cols[t]
        keep_mask = (slot_ids < live_all[t]).astype(jnp.float32)
        adjacency = counts_all[t].astype(jnp.float32) * keep_mask[:, None, None]
        return (global_row, global_col, adjacency, tile_col)

    def forward(state_pair, t):
        row_total, degree = state_pair
        global_row, global_col, adjacency, tile_col = tile_parts(t)
        product = jnp.einsum('kij,kjf->kif', adjacency, feat_blocks[global_col].astype(jnp.float32))
        row_total = row_total.at[global_row].add(product)
        degree = degree.at[global_row].add(lax.optimization_barrier(jnp.sum(adjacency, axis=2)))
        return ((row_total, degree), None)
    start_pair = (jnp.zeros((blocks_all, BS, F), jnp.float32), jnp.zeros((blocks_all, BS), jnp.float32))
    tile_ids = jnp.arange(tile_count, dtype=jnp.int32)
    (row_total, degree), _ = lax.scan(forward, start_pair, tile_ids)
    row_scale = lax.rsqrt(jnp.maximum(degree, 1.0))
    hidden = (row_total * row_scale[:, :, None]).reshape(NODES, F).astype(jnp.bfloat16)
    pre_act = jnp.dot(hidden, weight, preferred_element_type=jnp.float32) + bias
    layer_out = jax.nn.silu(pre_act).astype(jnp.bfloat16)
    pre_grad = (upstream.astype(jnp.float32) * silu_slope(pre_act)).astype(jnp.bfloat16)
    pulled = lax.dot_general(pre_grad, weight, (((1,), (1,)), ((), ())), preferred_element_type=jnp.float32)
    pulled = (pulled * row_scale.reshape(NODES, 1)).astype(jnp.bfloat16)
    pulled_blocks = pulled.reshape(blocks_all, BS, F)

    def backward(grad_blocks, t):
        global_row, global_col, adjacency, tile_col = tile_parts(t)
        product = jnp.einsum('kij,kif->kjf', adjacency, pulled_blocks[global_row].astype(jnp.float32))
        tile_term = jnp.zeros((COLB, BS, F), jnp.float32).at[tile_cols[t]].add(product)
        tile_term = lax.optimization_barrier(tile_term.astype(jnp.bfloat16)).astype(jnp.float32)
        col_base = (tile_col * COLB).astype(jnp.int32)
        current = lax.dynamic_slice_in_dim(grad_blocks, col_base, COLB, 0)
        grad_blocks = lax.dynamic_update_slice_in_dim(grad_blocks, current + tile_term, col_base, 0)
        return (grad_blocks, None)
    grad_blocks, _ = lax.scan(backward, jnp.zeros((blocks_all, BS, F), jnp.float32), tile_ids)
    account_grad = grad_blocks.reshape(NODES, F).astype(jnp.bfloat16)
    return (layer_out, account_grad)
```

```python
import functools

import jax
import jax.numpy as jnp
from jax import lax
from jax.experimental import pallas as pl
from jax.experimental.pallas import tpu as pltpu
from jax.sharding import PartitionSpec as P

LANES = 128
GROUP = 16
VMEM_BYTES = 60 * 1024 * 1024
f32 = jnp.float32
bf16 = jnp.bfloat16


def params(**kwargs):
    return pltpu.CompilerParams(vmem_limit_bytes=VMEM_BYTES, **kwargs)


def dot(a, b, dims):
    return lax.dot_general(a, b, (dims, ((), ())), preferred_element_type=f32)


def pack_rows(embed, target, devices, row_devs, col_devs, slot_cap):
    node_dev, feat_width = embed.shape
    slots = devices * slot_cap

    def body(embed_ref, trow_ref, tcol_ref, out_ref):
        def peer_of(t):
            shard = t // node_dev
            return shard % row_devs * col_devs + shard // row_devs

        trow = trow_ref[...]
        peer_row = peer_of(trow)
        peer_col = peer_of(tcol_ref[...])
        first = lax.broadcasted_iota(jnp.int32, (node_dev, node_dev), 0)
        second = lax.broadcasted_iota(jnp.int32, (node_dev, node_dev), 1)
        before = (peer_col == peer_row) & (first < second)
        rank = jnp.sum(jnp.where(before, 1, 0), axis=0, keepdims=True)
        slot = peer_row * slot_cap + rank
        hit = lax.broadcasted_iota(jnp.int32, (slots, node_dev), 0) == slot
        pick = jnp.where(hit, 1.0, 0.0).astype(bf16)
        out_ref[:, :feat_width] = dot(pick, embed_ref[...], ((1,), (0,))).astype(bf16)
        place = jnp.sum(jnp.where(hit, trow % node_dev + 1, 0), axis=1, keepdims=True)
        out_ref[:, feat_width:] = jnp.broadcast_to(place.astype(f32), (slots, LANES)).astype(bf16)

    return pl.pallas_call(
        body,
        out_shape=jax.ShapeDtypeStruct((slots, feat_width + LANES), bf16),
        compiler_params=params(),
        name="pack_rows",
    )(embed, target.reshape(1, node_dev), target.reshape(node_dev, 1))


def unpack_rows(rows_in, node_dev, feat_width):
    slots = rows_in.shape[0]

    def body(in_ref, out_ref):
        place = in_ref[:, feat_width:].astype(f32)
        place = jnp.concatenate([place] * (node_dev // LANES), axis=1)
        want = lax.broadcasted_iota(jnp.int32, (slots, node_dev), 1).astype(f32) + 1.0
        pick = jnp.where(place == want, 1.0, 0.0).astype(bf16)
        out_ref[...] = dot(pick, in_ref[:, :feat_width], ((0,), (0,))).astype(bf16)

    return pl.pallas_call(
        body,
        out_shape=jax.ShapeDtypeStruct((node_dev, feat_width), bf16),
        compiler_params=params(),
        name="unpack_rows",
    )(rows_in)


def live_groups(live_ref):
    return (live_ref[0] + GROUP - 1) // GROUP


def group_map(g, live_ref, *_):
    return (jnp.minimum(g, jnp.maximum(live_groups(live_ref) - 1, 0)), 0, 0)


def prepare(counts, tile_rows, live, row_blocks):
    slot_total, side, _ = counts.shape

    def body(live_ref, rows_ref, counts_ref, adj_ref, adjt_ref, deg_ref):
        g = pl.program_id(0)

        @pl.when(g == 0)
        def _():
            deg_ref[...] = jnp.zeros_like(deg_ref)

        @pl.when(g < live_groups(live_ref))
        def _():
            ones = jnp.ones((side, LANES), bf16)
            for j in range(GROUP):
                slot = g * GROUP + j
                keep = jnp.where(slot < live_ref[0], 1.0, 0.0)
                block = counts_ref[j].astype(f32) * keep
                adj = block.astype(bf16)
                adj_ref[j] = adj
                adjt_ref[j] = block.T.astype(bf16)
                start = pl.multiple_of(rows_ref[slot] * side, side)
                deg_ref[pl.ds(start, side), :] += dot(adj, ones, ((1,), (0,)))

    block = pl.BlockSpec((GROUP, side, side), group_map)
    return pl.pallas_call(
        body,
        grid_spec=pltpu.PrefetchScalarGridSpec(
            num_scalar_prefetch=2,
            grid=(slot_total // GROUP,),
            in_specs=[block],
            out_specs=[block, block, pl.BlockSpec((row_blocks * side, LANES), lambda g, *_: (0, 0))],
        ),
        out_shape=[
            jax.ShapeDtypeStruct(counts.shape, bf16),
            jax.ShapeDtypeStruct(counts.shape, bf16),
            jax.ShapeDtypeStruct((row_blocks * side, LANES), f32),
        ],
        compiler_params=params(),
        name="prepare",
    )(live, tile_rows, counts)


def block_product(adj, values, out_pick, in_pick, live, out_pieces, name):
    slot_total, side, _ = adj.shape
    piece = values[0].shape
    groups = slot_total // GROUP
    count = len(values)

    def body(live_ref, out_pick_ref, in_pick_ref, adj_ref, *refs):
        val_refs = refs[:count]
        out_refs = refs[count : count + out_pieces]
        val_ref, acc_ref, sems = refs[count + out_pieces :]
        g = pl.program_id(0)

        @pl.when(g == 0)
        def _():
            copies = [
                pltpu.make_async_copy(ref, val_ref.at[pl.ds(k * piece[0], piece[0]), :], sems.at[k])
                for k, ref in enumerate(val_refs)
            ]
            for c in copies:
                c.start()
            acc_ref[...] = jnp.zeros_like(acc_ref)
            for c in copies:
                c.wait()

        @pl.when(g < live_groups(live_ref))
        def _():
            for j in range(GROUP):
                slot = g * GROUP + j
                src = pl.multiple_of(in_pick_ref[slot] * side, side)
                dst = pl.multiple_of(out_pick_ref[slot] * side, side)
                acc_ref[pl.ds(dst, side), :] += dot(adj_ref[j], val_ref[pl.ds(src, side), :], ((1,), (0,)))

        @pl.when(g == groups - 1)
        def _():
            for k, ref in enumerate(out_refs):
                ref[...] = acc_ref[k * piece[0] : (k + 1) * piece[0], :].astype(bf16)

    whole = pl.BlockSpec(piece, lambda g, *_: (0, 0), pipeline_mode=pl.Buffered(1))
    return pl.pallas_call(
        body,
        grid_spec=pltpu.PrefetchScalarGridSpec(
            num_scalar_prefetch=3,
            grid=(groups,),
            in_specs=[pl.BlockSpec((GROUP, side, side), group_map)] + [pl.BlockSpec(memory_space=pl.ANY)] * count,
            out_specs=[whole] * out_pieces,
            scratch_shapes=[
                pltpu.VMEM((count * piece[0], piece[1]), bf16),
                pltpu.VMEM((out_pieces * piece[0], piece[1]), f32),
                pltpu.SemaphoreType.DMA((count,)),
            ],
        ),
        out_shape=[jax.ShapeDtypeStruct(piece, bf16)] * out_pieces,
        compiler_params=params(),
        name=name,
    )(live, out_pick, in_pick, adj, *values)


def swap(x, axis, k):
    size = lax.axis_size(axis)
    return lax.ppermute(x, axis, [(i, i ^ k) for i in range(size)])


def dense_part(parts, degree, weight, bias, upstream, col):
    col_devs = len(parts)
    rows, feat_width = parts[0].shape

    def body(col_ref, deg_ref, w_ref, b_ref, up_ref, *refs):
        parts_refs, (out_ref, pulled_ref) = refs[:col_devs], refs[col_devs:]
        total = parts_refs[0][...].astype(f32)
        for ref in parts_refs[1:]:
            total = total + ref[...].astype(f32)
        deg = jnp.sum(deg_ref[...], axis=1, keepdims=True)
        row_scale = lax.rsqrt(jnp.maximum(deg, 1.0))
        hidden = (total * row_scale).astype(bf16)
        w = w_ref[...]
        pre_act = dot(hidden, w, ((1,), (0,))) + b_ref[...]
        logistic = jax.nn.sigmoid(pre_act)
        out_ref[...] = (pre_act * logistic).astype(bf16)
        slope = logistic * (1.0 + pre_act * (1.0 - logistic))
        pre_grad = (up_ref[...].astype(f32) * slope).astype(bf16)
        pulled = dot(pre_grad, w, ((1,), (1,)))
        pulled_ref[...] = (pulled * row_scale).astype(bf16)

    full = lambda shape: pl.BlockSpec(shape, lambda i, c: (0,) * len(shape))
    out = jax.ShapeDtypeStruct((rows, feat_width), bf16)
    return pl.pallas_call(
        body,
        grid_spec=pltpu.PrefetchScalarGridSpec(
            num_scalar_prefetch=1,
            grid=(1,),
            in_specs=[
                full(degree.shape),
                full(weight.shape),
                full((1, feat_width)),
                pl.BlockSpec((rows, feat_width), lambda i, c: (c[0], 0)),
            ]
            + [full((rows, feat_width))] * col_devs,
            out_specs=[full((rows, feat_width))] * 2,
        ),
        out_shape=[out, out],
        compiler_params=params(),
        name="dense_part",
    )(col, degree, weight, bias.reshape(1, feat_width), upstream, *parts)


def per_device(embed, target, weight, bias, block_row, block_col, block_live, edge_count, upstream):
    node_dev, feat_width = embed.shape
    side = edge_count.shape[3]
    slot_total = edge_count.shape[2]
    row_devs = lax.axis_size("row")
    col_devs = lax.axis_size("col")
    devices = row_devs * col_devs
    slot_cap = 2 * (node_dev // devices) - 1
    row_blocks = col_devs * node_dev // side
    per_dev = node_dev // side
    row = lax.axis_index("row").astype(jnp.int32)
    col = lax.axis_index("col").astype(jnp.int32)
    counts = edge_count.reshape(slot_total, side, side)
    tile_rows = block_row.reshape(slot_total) ^ (col * per_dev)
    tile_cols = block_col.reshape(slot_total) ^ (row * per_dev)
    live = block_live.reshape(1)

    send = pack_rows(embed, target, devices, row_devs, col_devs, slot_cap)
    rows_in = lax.all_to_all(
        send.reshape(devices, slot_cap, -1), ("row", "col"), split_axis=0, concat_axis=0, tiled=True
    )
    own_rows = unpack_rows(rows_in.reshape(devices * slot_cap, -1), node_dev, feat_width)

    adj, adjt, deg = prepare(counts, tile_rows, live, row_blocks)
    deg = deg[:, 0].reshape(col_devs, node_dev)
    deg_parts = [deg[0]] + [swap(deg[k], "col", k) for k in range(1, col_devs)]
    deg_parts = jnp.stack(deg_parts, axis=1)

    feats = [None] * row_devs
    for k in range(0, row_devs, 2):
        feats[k] = own_rows if k == 0 else swap(own_rows, "row", k)
    for k in range(0, row_devs, 2):
        feats[k + 1] = swap(feats[k], "row", 1)
    row_part = block_product(adj, feats, tile_rows, tile_cols, live, col_devs, "forward")
    parts = [row_part[0]] + [swap(row_part[k], "col", k) for k in range(1, col_devs)]
    layer_out, pulled = dense_part(parts, deg_parts, weight, bias, upstream, col.reshape(1))
    row_pulled = [pulled] + [swap(pulled, "col", k) for k in range(1, col_devs)]
    col_term = block_product(adjt, row_pulled, tile_cols, tile_rows, live, row_devs, "backward")
    pair_sum = [
        (col_term[k].astype(f32) + swap(col_term[k + 1], "row", 1).astype(f32)).astype(bf16)
        for k in range(0, row_devs, 2)
    ]
    total = pair_sum[0].astype(f32)
    for k in range(1, row_devs // 2):
        total = total + swap(pair_sum[k], "row", 2 * k).astype(f32)
    return (layer_out, total.astype(bf16))


def solution(mesh):
    in_specs = (
        P(("row", "col"), None),
        P(("row", "col")),
        P(),
        P(),
        P("row", "col", None),
        P("row", "col", None),
        P("row", "col"),
        P("row", "col", None, None, None),
        P("row", None),
    )
    out_specs = (P(("row", "col"), None), P(("col", "row"), None))
    return jax.shard_map(
        per_device, mesh=mesh, in_specs=in_specs, out_specs=out_specs, check_vma=False
    )
```

```python
import functools

import jax
import jax.numpy as jnp
from jax import lax
from jax.experimental import pallas as pl
from jax.experimental.pallas import tpu as pltpu
from jax.sharding import PartitionSpec as P

LANES = 128
GROUP = 16
VMEM_BYTES = 60 * 1024 * 1024
f32 = jnp.float32
bf16 = jnp.bfloat16


def params(**kwargs):
    return pltpu.CompilerParams(vmem_limit_bytes=VMEM_BYTES, **kwargs)


def dot(a, b, dims):
    return lax.dot_general(a, b, (dims, ((), ())), preferred_element_type=f32)


def pack_rows(embed, target, devices, row_devs, col_devs, slot_cap):
    node_dev, feat_width = embed.shape
    block = slot_cap + 1
    slots = devices * block

    def body(embed_ref, trow_ref, out_ref):
        trow = jnp.broadcast_to(trow_ref[...], (node_dev, node_dev))
        tcol = trow.T

        def peer_of(t):
            shard = t // node_dev
            return shard % row_devs * col_devs + shard // row_devs

        peer_row = peer_of(trow)
        first = lax.broadcasted_iota(jnp.int32, (node_dev, node_dev), 0)
        second = lax.broadcasted_iota(jnp.int32, (node_dev, node_dev), 1)
        before = (peer_of(tcol) == peer_row) & (first < second)
        rank = jnp.sum(jnp.where(before, 1, 0), axis=0, keepdims=True)
        base = peer_row[:1] * block
        row_id = lax.broadcasted_iota(jnp.int32, (slots, node_dev), 0)
        pick = jnp.where(row_id == base + rank, 1.0, 0.0).astype(bf16)
        rows = dot(pick, embed_ref[...], ((1,), (0,)))
        place = (tcol % node_dev + 1).astype(f32)[:, :LANES].astype(bf16)
        last = row_id == base + slot_cap
        places = [
            dot(jnp.where(last & (rank == r), 1.0, 0.0).astype(bf16), place, ((1,), (0,))) for r in range(slot_cap)
        ]
        places.append(jnp.zeros((slots, feat_width - slot_cap * LANES), f32))
        out_ref[...] = (rows + jnp.concatenate(places, axis=1)).astype(bf16)

    return pl.pallas_call(
        body,
        out_shape=jax.ShapeDtypeStruct((slots, feat_width), bf16),
        compiler_params=params(),
        name="pack_rows",
    )(embed, target.reshape(1, node_dev))


def unpack_rows(rows_in, node_dev, slot_cap):
    slots, feat_width = rows_in.shape
    block = slot_cap + 1

    def body(in_ref, out_ref):
        kind = lax.broadcasted_iota(jnp.int32, (slots, LANES), 0) % block
        place = jnp.zeros((slots, LANES), f32)
        for r in range(slot_cap):
            held = in_ref[:, r * LANES : (r + 1) * LANES].astype(f32)
            place = jnp.where(kind == r, pltpu.roll(held, slots - (slot_cap - r), 0), place)
        place = jnp.concatenate([place] * (node_dev // LANES), axis=1)
        want = lax.broadcasted_iota(jnp.int32, (slots, node_dev), 1).astype(f32) + 1.0
        pick = jnp.where(place == want, 1.0, 0.0).astype(bf16)
        out_ref[...] = dot(pick, in_ref[...], ((0,), (0,))).astype(bf16)

    return pl.pallas_call(
        body,
        out_shape=jax.ShapeDtypeStruct((node_dev, feat_width), bf16),
        compiler_params=params(),
        name="unpack_rows",
    )(rows_in)


def live_groups(live_ref):
    return (live_ref[0] + GROUP - 1) // GROUP


def group_map(g, live_ref, *_):
    return (jnp.minimum(g, jnp.maximum(live_groups(live_ref) - 1, 0)), 0, 0)


def prepare(counts, tile_rows, live, row_blocks):
    slot_total, side, _ = counts.shape

    def body(live_ref, rows_ref, counts_ref, adj_ref, adjt_ref, deg_ref):
        g = pl.program_id(0)

        @pl.when(g == 0)
        def _():
            deg_ref[...] = jnp.zeros_like(deg_ref)

        @pl.when(g < live_groups(live_ref))
        def _():
            ones = jnp.ones((side, LANES), bf16)
            for j in range(GROUP):
                slot = g * GROUP + j
                keep = jnp.where(slot < live_ref[0], 1.0, 0.0)
                block = counts_ref[j].astype(f32) * keep
                adj = block.astype(bf16)
                adj_ref[j] = adj
                adjt_ref[j] = block.T.astype(bf16)
                start = pl.multiple_of(rows_ref[slot] * side, side)
                deg_ref[pl.ds(start, side), :] += dot(adj, ones, ((1,), (0,)))

    block = pl.BlockSpec((GROUP, side, side), group_map)
    return pl.pallas_call(
        body,
        grid_spec=pltpu.PrefetchScalarGridSpec(
            num_scalar_prefetch=2,
            grid=(slot_total // GROUP,),
            in_specs=[block],
            out_specs=[block, block, pl.BlockSpec((row_blocks * side, LANES), lambda g, *_: (0, 0))],
        ),
        out_shape=[
            jax.ShapeDtypeStruct(counts.shape, bf16),
            jax.ShapeDtypeStruct(counts.shape, bf16),
            jax.ShapeDtypeStruct((row_blocks * side, LANES), f32),
        ],
        compiler_params=params(),
        name="prepare",
    )(live, tile_rows, counts)


def block_product(adj, values, out_pick, in_pick, live, out_rows, name):
    slot_total, side, _ = adj.shape
    feat_width = values[0].shape[1]
    groups = slot_total // GROUP
    count = len(values)

    def body(live_ref, out_pick_ref, in_pick_ref, adj_hbm, *refs):
        val_hbm = refs[:count]
        out_refs = refs[count : count + len(out_rows)]
        val_ref, adj_ref, acc_ref, val_sems, adj_sems = refs[count + len(out_rows) :]
        live_count = live_groups(live_ref)

        def adj_copy(g):
            part = pl.ds(g * GROUP, GROUP)
            return pltpu.make_async_copy(adj_hbm.at[part], adj_ref.at[part], adj_sems.at[g])

        copies = []
        start = 0
        for k, ref in enumerate(val_hbm):
            rows = ref.shape[0]
            copies.append(pltpu.make_async_copy(ref, val_ref.at[pl.ds(start, rows), :], val_sems.at[k]))
            start += rows
        for c in copies:
            c.start()
        lax.fori_loop(0, live_count, lambda g, _: (adj_copy(g).start(), 0)[1], 0)
        acc_ref[...] = jnp.zeros_like(acc_ref)
        for c in copies:
            c.wait()

        def group(g, _):
            adj_copy(g).wait()
            for j in range(GROUP):
                slot = g * GROUP + j
                src = pl.multiple_of(in_pick_ref[slot] * side, side)
                dst = pl.multiple_of(out_pick_ref[slot] * side, side)
                acc_ref[pl.ds(dst, side), :] += dot(adj_ref[slot], val_ref[pl.ds(src, side), :], ((1,), (0,)))
            return 0

        lax.fori_loop(0, live_count, group, 0)
        start = 0
        for ref, rows in zip(out_refs, out_rows):
            ref[...] = acc_ref[start : start + rows, :].astype(bf16)
            start += rows

    return pl.pallas_call(
        body,
        grid_spec=pltpu.PrefetchScalarGridSpec(
            num_scalar_prefetch=3,
            grid=(),
            in_specs=[pl.BlockSpec(memory_space=pl.ANY)] * (count + 1),
            out_specs=[pl.BlockSpec(memory_space=pltpu.VMEM)] * len(out_rows),
            scratch_shapes=[
                pltpu.VMEM((sum(v.shape[0] for v in values), feat_width), bf16),
                pltpu.VMEM(adj.shape, bf16),
                pltpu.VMEM((sum(out_rows), feat_width), f32),
                pltpu.SemaphoreType.DMA((count,)),
                pltpu.SemaphoreType.DMA((groups,)),
            ],
        ),
        out_shape=[jax.ShapeDtypeStruct((rows, feat_width), bf16) for rows in out_rows],
        compiler_params=params(),
        name=name,
    )(live, out_pick, in_pick, adj, *values)


def swap(x, axis, k):
    size = lax.axis_size(axis)
    return lax.ppermute(x, axis, [(i, i ^ k) for i in range(size)])


def dense_part(parts, degree, weight, bias, upstream, col):
    col_devs = len(parts)
    rows, feat_width = parts[0].shape

    def body(col_ref, deg_ref, w_ref, b_ref, up_ref, *refs):
        parts_refs, (out_ref, pulled_ref) = refs[:col_devs], refs[col_devs:]
        total = parts_refs[0][...].astype(f32)
        for ref in parts_refs[1:]:
            total = total + ref[...].astype(f32)
        deg = jnp.sum(deg_ref[...], axis=1, keepdims=True)
        row_scale = lax.rsqrt(jnp.maximum(deg, 1.0))
        hidden = (total * row_scale).astype(bf16)
        w = w_ref[...]
        pre_act = dot(hidden, w, ((1,), (0,))) + b_ref[...]
        logistic = jax.nn.sigmoid(pre_act)
        out_ref[...] = (pre_act * logistic).astype(bf16)
        slope = logistic * (1.0 + pre_act * (1.0 - logistic))
        pre_grad = (up_ref[...].astype(f32) * slope).astype(bf16)
        pulled = dot(pre_grad, w, ((1,), (1,)))
        pulled_ref[...] = (pulled * row_scale).astype(bf16)

    full = lambda shape: pl.BlockSpec(shape, lambda i, c: (0,) * len(shape))
    out = jax.ShapeDtypeStruct((rows, feat_width), bf16)
    return pl.pallas_call(
        body,
        grid_spec=pltpu.PrefetchScalarGridSpec(
            num_scalar_prefetch=1,
            grid=(1,),
            in_specs=[
                full(degree.shape),
                full(weight.shape),
                full((1, feat_width)),
                pl.BlockSpec((rows, feat_width), lambda i, c: (c[0], 0)),
            ]
            + [full((rows, feat_width))] * col_devs,
            out_specs=[full((rows, feat_width))] * 2,
        ),
        out_shape=[out, out],
        compiler_params=params(),
        name="dense_part",
    )(col, degree, weight, bias.reshape(1, feat_width), upstream, *parts)


def per_device(embed, target, weight, bias, block_row, block_col, block_live, edge_count, upstream):
    node_dev, feat_width = embed.shape
    side = edge_count.shape[3]
    slot_total = edge_count.shape[2]
    row_devs = lax.axis_size("row")
    col_devs = lax.axis_size("col")
    devices = row_devs * col_devs
    slot_cap = 2 * (node_dev // devices) - 1
    row_blocks = col_devs * node_dev // side
    per_dev = node_dev // side
    row = lax.axis_index("row").astype(jnp.int32)
    col = lax.axis_index("col").astype(jnp.int32)
    counts = edge_count.reshape(slot_total, side, side)
    live = block_live.reshape(1)
    half = node_dev // 2
    tile_rows = block_row.reshape(slot_total) ^ (col * per_dev)
    col_dist = block_col.reshape(slot_total) ^ (row * per_dev)
    dist = col_dist // per_dev
    tile_cols = ((dist % 2) * (row_devs // 2) + dist // 2) * per_dev + col_dist % per_dev

    send = pack_rows(embed, target, devices, row_devs, col_devs, slot_cap)
    rows_in = lax.all_to_all(
        send.reshape(devices, slot_cap + 1, feat_width), ("row", "col"), split_axis=0, concat_axis=0, tiled=True
    )

    adj, adjt, deg = prepare(counts, tile_rows, live, row_blocks)
    deg = deg[:, 0].reshape(col_devs, node_dev)
    deg_parts = [deg[0]] + [swap(deg[k], "col", k) for k in range(1, col_devs)]
    deg_parts = jnp.stack(deg_parts, axis=1)
    rows_in, deg_parts, adj, adjt = lax.optimization_barrier((rows_in, deg_parts, adj, adjt))
    own_rows = unpack_rows(rows_in.reshape(devices * (slot_cap + 1), feat_width), node_dev, slot_cap)

    def y_gather(x):
        near = swap(x, "row", 4)
        wrap = swap(x, "row", 12)
        return [x], [near], [swap(wrap[:half], "row", 4), swap(near[half:], "row", 12)], [wrap]

    z_rows = swap(own_rows, "row", 2)
    here = y_gather(own_rows)
    there = y_gather(z_rows)
    feats = [p for pair in zip(here, there) for pieces in pair for p in pieces]
    feats = feats + [swap(p, "row", 1) for p in feats]
    row_part = block_product(adj, feats, tile_rows, tile_cols, live, [node_dev] * col_devs, "forward")
    parts = [row_part[0]] + [swap(row_part[k], "col", k) for k in range(1, col_devs)]
    layer_out, pulled = dense_part(parts, deg_parts, weight, bias, upstream, col.reshape(1))
    row_pulled = [pulled] + [swap(pulled, "col", k) for k in range(1, col_devs)]
    chips = row_devs // 2
    col_term = block_product(
        adjt, row_pulled, tile_cols, tile_rows, live, [node_dev] * chips + [node_dev * chips // 2] * 2, "backward"
    )
    other = [swap(col_term[chips], "row", 1), swap(col_term[chips + 1], "row", 1)]
    pair_sum = []
    for k in range(chips):
        start = (k % (chips // 2)) * node_dev
        got = other[k // (chips // 2)][start : start + node_dev]
        pair_sum.append((col_term[k].astype(f32) + got.astype(f32)).astype(bf16))
    total = pair_sum[0].astype(f32)
    for k in range(1, chips):
        total = total + swap(pair_sum[k], "row", 2 * k).astype(f32)
    return (layer_out, total.astype(bf16))


def solution(mesh):
    in_specs = (
        P(("row", "col"), None),
        P(("row", "col")),
        P(),
        P(),
        P("row", "col", None),
        P("row", "col", None),
        P("row", "col"),
        P("row", "col", None, None, None),
        P("row", None),
    )
    out_specs = (P(("row", "col"), None), P(("col", "row"), None))
    return jax.shard_map(
        per_device, mesh=mesh, in_specs=in_specs, out_specs=out_specs, check_vma=False
    )
```

```python
import functools

import jax
import jax.numpy as jnp
from jax import lax
from jax.experimental import pallas as pl
from jax.experimental.pallas import tpu as pltpu
from jax.sharding import PartitionSpec as P

LANES = 128
GROUP = 16
DEG_ROWS = 16
VMEM_BYTES = 60 * 1024 * 1024
f32 = jnp.float32
bf16 = jnp.bfloat16


def params(**kwargs):
    return pltpu.CompilerParams(vmem_limit_bytes=VMEM_BYTES, **kwargs)


def dot(a, b, dims):
    return lax.dot_general(a, b, (dims, ((), ())), preferred_element_type=f32)


def pack_rows(embed, target, devices, row_devs, col_devs, slot_cap):
    node_dev, feat_width = embed.shape
    block = slot_cap + 1
    slots = devices * block

    def body(embed_ref, trow_ref, out_ref):
        trow = jnp.broadcast_to(trow_ref[...], (node_dev, node_dev))
        tcol = trow.T

        def peer_of(t):
            shard = t // node_dev
            return shard % row_devs * col_devs + shard // row_devs

        peer_row = peer_of(trow)
        first = lax.broadcasted_iota(jnp.int32, (node_dev, node_dev), 0)
        second = lax.broadcasted_iota(jnp.int32, (node_dev, node_dev), 1)
        before = (peer_of(tcol) == peer_row) & (first < second)
        rank = jnp.sum(jnp.where(before, 1, 0), axis=0, keepdims=True)
        base = peer_row[:1] * block
        row_id = lax.broadcasted_iota(jnp.int32, (slots, node_dev), 0)
        pick = jnp.where(row_id == base + rank, 1.0, 0.0).astype(bf16)
        rows = dot(pick, embed_ref[...], ((1,), (0,)))
        place = (tcol % node_dev + 1).astype(f32)[:, :LANES].astype(bf16)
        last = row_id == base + slot_cap
        places = [
            dot(jnp.where(last & (rank == r), 1.0, 0.0).astype(bf16), place, ((1,), (0,))) for r in range(slot_cap)
        ]
        places.append(jnp.zeros((slots, feat_width - slot_cap * LANES), f32))
        out_ref[...] = (rows + jnp.concatenate(places, axis=1)).astype(bf16)

    return pl.pallas_call(
        body,
        out_shape=jax.ShapeDtypeStruct((slots, feat_width), bf16),
        compiler_params=params(),
        name="pack_rows",
    )(embed, target.reshape(1, node_dev))


def unpack_rows(rows_in, node_dev, slot_cap):
    slots, feat_width = rows_in.shape
    block = slot_cap + 1

    def body(in_ref, out_ref):
        kind = lax.broadcasted_iota(jnp.int32, (slots, LANES), 0) % block
        place = jnp.zeros((slots, LANES), f32)
        for r in range(slot_cap):
            held = in_ref[:, r * LANES : (r + 1) * LANES].astype(f32)
            place = jnp.where(kind == r, pltpu.roll(held, slots - (slot_cap - r), 0), place)
        place = jnp.concatenate([place] * (node_dev // LANES), axis=1)
        want = lax.broadcasted_iota(jnp.int32, (slots, node_dev), 1).astype(f32) + 1.0
        pick = jnp.where(place == want, 1.0, 0.0).astype(bf16)
        out_ref[...] = dot(pick, in_ref[...], ((0,), (0,))).astype(bf16)

    return pl.pallas_call(
        body,
        out_shape=jax.ShapeDtypeStruct((node_dev, feat_width), bf16),
        compiler_params=params(),
        name="unpack_rows",
    )(rows_in)


def live_groups(live_ref):
    return (live_ref[0] + GROUP - 1) // GROUP


def group_map(g, live_ref, *_):
    return (jnp.minimum(g, jnp.maximum(live_groups(live_ref) - 1, 0)), 0, 0)


def prepare(counts, tile_rows, live, row_blocks):
    slot_total, side, _ = counts.shape

    def body(live_ref, rows_ref, counts_ref, adj_ref, adjt_ref, deg_ref):
        g = pl.program_id(0)

        @pl.when(g == 0)
        def _():
            deg_ref[...] = jnp.zeros_like(deg_ref)

        @pl.when(g < live_groups(live_ref))
        def _():
            ones = jnp.ones((8, side), bf16)
            for j in range(GROUP):
                slot = g * GROUP + j
                keep = jnp.where(slot < live_ref[0], 1.0, 0.0)
                block = counts_ref[j].astype(f32) * keep
                adj_ref[j] = block.astype(bf16)
                adjt = block.T.astype(bf16)
                adjt_ref[j] = adjt
                start = pl.multiple_of(rows_ref[slot] * 8, 8)
                deg_ref[pl.ds(start, 8), :] += dot(ones, adjt, ((1,), (0,)))

    block = pl.BlockSpec((GROUP, side, side), group_map)
    return pl.pallas_call(
        body,
        grid_spec=pltpu.PrefetchScalarGridSpec(
            num_scalar_prefetch=2,
            grid=(slot_total // GROUP,),
            in_specs=[block],
            out_specs=[block, block, pl.BlockSpec((row_blocks * 8, side), lambda g, *_: (0, 0))],
        ),
        out_shape=[
            jax.ShapeDtypeStruct(counts.shape, bf16),
            jax.ShapeDtypeStruct(counts.shape, bf16),
            jax.ShapeDtypeStruct((row_blocks * 8, side), f32),
        ],
        compiler_params=params(),
        name="prepare",
    )(live, tile_rows, counts)


def block_product(adj, values, out_pick, in_pick, live, out_rows, name, degree=None):
    slot_total, side, _ = adj.shape
    feat_width = values[0].shape[1]
    groups = slot_total // GROUP
    count = len(values)
    tails = [] if degree is None else [degree]

    def body(live_ref, out_pick_ref, in_pick_ref, *refs):
        deg_refs, adj_hbm, refs = refs[: len(tails)], refs[len(tails)], refs[len(tails) + 1 :]
        val_hbm = refs[:count]
        out_refs = refs[count : count + len(out_rows)]
        val_ref, adj_ref, acc_ref, val_sems, adj_sems = refs[count + len(out_rows) :]
        live_count = live_groups(live_ref)

        def adj_copy(g):
            part = pl.ds(g * GROUP, GROUP)
            return pltpu.make_async_copy(adj_hbm.at[part], adj_ref.at[part], adj_sems.at[g])

        copies = []
        start = 0
        for k, ref in enumerate(val_hbm):
            rows = ref.shape[0]
            copies.append(pltpu.make_async_copy(ref, val_ref.at[pl.ds(start, rows), :], val_sems.at[k]))
            start += rows
        for c in copies:
            c.start()
        lax.fori_loop(0, live_count, lambda g, _: (adj_copy(g).start(), 0)[1], 0)
        acc_ref[...] = jnp.zeros_like(acc_ref)
        for c in copies:
            c.wait()

        def group(g, _):
            adj_copy(g).wait()
            for j in range(GROUP):
                slot = g * GROUP + j
                src = pl.multiple_of(in_pick_ref[slot] * side, side)
                dst = pl.multiple_of(out_pick_ref[slot] * side, side)
                acc_ref[pl.ds(dst, side), :] += dot(adj_ref[slot], val_ref[pl.ds(src, side), :], ((1,), (0,)))
            return 0

        lax.fori_loop(0, live_count, group, 0)
        start = 0
        for k, (ref, rows) in enumerate(zip(out_refs, out_rows)):
            ref[:rows, :] = acc_ref[start : start + rows, :].astype(bf16)
            start += rows
            for deg_ref in deg_refs:
                blocks = rows // side
                deg = [deg_ref[(k * blocks + i) * 8 : (k * blocks + i + 1) * 8, :] for i in range(blocks)]
                deg = jnp.concatenate(deg, axis=1)
                high = jnp.floor(deg * (1.0 / 32.0))
                top = jnp.floor(high * (1.0 / 32.0))
                low = jnp.concatenate([deg - 32.0 * high, high - 32.0 * top], axis=1)
                rest = jnp.concatenate([top, jnp.zeros_like(top)], axis=1)
                ref[rows:, :] = jnp.concatenate([low, rest], axis=0).astype(bf16)

    return pl.pallas_call(
        body,
        grid_spec=pltpu.PrefetchScalarGridSpec(
            num_scalar_prefetch=3,
            grid=(),
            in_specs=[pl.BlockSpec(memory_space=pltpu.VMEM)] * len(tails)
            + [pl.BlockSpec(memory_space=pl.ANY)] * (count + 1),
            out_specs=[pl.BlockSpec(memory_space=pltpu.VMEM)] * len(out_rows),
            scratch_shapes=[
                pltpu.VMEM((sum(v.shape[0] for v in values), feat_width), bf16),
                pltpu.VMEM(adj.shape, bf16),
                pltpu.VMEM((sum(out_rows), feat_width), f32),
                pltpu.SemaphoreType.DMA((count,)),
                pltpu.SemaphoreType.DMA((groups,)),
            ],
        ),
        out_shape=[jax.ShapeDtypeStruct((rows + DEG_ROWS * len(tails), feat_width), bf16) for rows in out_rows],
        compiler_params=params(),
        name=name,
    )(live, out_pick, in_pick, *tails, adj, *values)


def swap(x, axis, k):
    size = lax.axis_size(axis)
    return lax.ppermute(x, axis, [(i, i ^ k) for i in range(size)])


def dense_part(parts, weight, bias, upstream, col):
    count = len(parts)
    rows, feat_width = parts[0].shape[0] - DEG_ROWS, parts[0].shape[1]

    def body(col_ref, w_ref, b_ref, up_ref, *refs):
        parts_refs, (out_ref, pulled_ref) = refs[:count], refs[count:]
        total = parts_refs[0][...].astype(f32)
        for ref in parts_refs[1:]:
            total = total + ref[...].astype(f32)
        digits = total[rows:, :]
        total = total[:rows, :]
        deg = digits[:1, :rows] + 32.0 * digits[:1, rows : 2 * rows] + 1024.0 * digits[8:9, :rows]
        deg = jnp.broadcast_to(deg, (LANES, rows)).T
        deg = jnp.concatenate([deg] * (feat_width // LANES), axis=1)
        row_scale = lax.rsqrt(jnp.maximum(deg, 1.0))
        hidden = (total * row_scale).astype(bf16)
        w = w_ref[...]
        pre_act = dot(hidden, w, ((1,), (0,))) + b_ref[...]
        logistic = jax.nn.sigmoid(pre_act)
        out_ref[...] = (pre_act * logistic).astype(bf16)
        slope = logistic * (1.0 + pre_act * (1.0 - logistic))
        pre_grad = (up_ref[...].astype(f32) * slope).astype(bf16)
        pulled = dot(pre_grad, w, ((1,), (1,)))
        pulled_ref[...] = (pulled * row_scale).astype(bf16)

    full = lambda shape: pl.BlockSpec(shape, lambda i, c: (0,) * len(shape))
    out = jax.ShapeDtypeStruct((rows, feat_width), bf16)
    return pl.pallas_call(
        body,
        grid_spec=pltpu.PrefetchScalarGridSpec(
            num_scalar_prefetch=1,
            grid=(1,),
            in_specs=[
                full(weight.shape),
                full((1, feat_width)),
                pl.BlockSpec((rows, feat_width), lambda i, c: (c[0], 0)),
            ]
            + [full(parts[0].shape)] * count,
            out_specs=[full((rows, feat_width))] * 2,
        ),
        out_shape=[out, out],
        compiler_params=params(),
        name="dense_part",
    )(col, weight, bias.reshape(1, feat_width), upstream, *parts)


def add(*terms):
    total = terms[0].astype(f32)
    for t in terms[1:]:
        total = total + t.astype(f32)
    return total.astype(bf16)


def plane_gather(x, axis, near, far_near, z):
    x_z = swap(x, axis, z)
    one, one_z = swap(x, axis, near), swap(x_z, axis, near)
    three, three_z = swap(x, axis, far_near), swap(x_z, axis, far_near)
    two, two_z = swap(three, axis, near), swap(one_z, axis, far_near)
    return [x, x_z, one, one_z, two, two_z, three, three_z]


def plane_reduce(p, axis, near, far_near, z):
    two_z = swap(p[5], axis, far_near)
    two = swap(p[4], axis, near)
    three_z = swap(p[7], axis, far_near)
    one_z = swap(add(p[3], two_z), axis, near)
    one = swap(p[2], axis, near)
    over_z = swap(add(p[1], three_z, one_z), axis, z)
    three = swap(add(p[6], two), axis, far_near)
    return [p[0], one, three, over_z]


def per_device(embed, target, weight, bias, block_row, block_col, block_live, edge_count, upstream):
    node_dev, feat_width = embed.shape
    side = edge_count.shape[3]
    slot_total = edge_count.shape[2]
    row_devs = lax.axis_size("row")
    col_devs = lax.axis_size("col")
    devices = row_devs * col_devs
    slot_cap = 2 * (node_dev // devices) - 1
    row_blocks = col_devs * node_dev // side
    per_dev = node_dev // side
    row = lax.axis_index("row").astype(jnp.int32)
    col = lax.axis_index("col").astype(jnp.int32)
    counts = edge_count.reshape(slot_total, side, side)
    live = block_live.reshape(1)
    tile_rows = block_row.reshape(slot_total) ^ (col * per_dev)
    col_dist = block_col.reshape(slot_total) ^ (row * per_dev)
    dist = col_dist // per_dev
    tile_cols = ((dist % 2) * (row_devs // 2) + dist // 2) * per_dev + col_dist % per_dev

    send = pack_rows(embed, target, devices, row_devs, col_devs, slot_cap)
    rows_in = lax.all_to_all(
        send.reshape(devices, slot_cap + 1, feat_width), ("row", "col"), split_axis=0, concat_axis=0, tiled=True
    )

    adj, adjt, deg = prepare(counts, tile_rows, live, row_blocks)
    rows_in, deg, adj, adjt = lax.optimization_barrier((rows_in, deg, adj, adjt))
    own_rows = unpack_rows(rows_in.reshape(devices * (slot_cap + 1), feat_width), node_dev, slot_cap)

    feats = plane_gather(own_rows, "row", 4, 12, 2)
    feats = feats + [swap(p, "row", 1) for p in feats]
    row_part = block_product(adj, feats, tile_rows, tile_cols, live, [node_dev] * col_devs, "forward", deg)
    parts = plane_reduce(row_part, "col", 2, 6, 1)
    layer_out, pulled = dense_part(parts, weight, bias, upstream, col.reshape(1))
    row_pulled = plane_gather(pulled, "col", 2, 6, 1)
    chips = row_devs // 2
    col_term = block_product(
        adjt, row_pulled, tile_cols, tile_rows, live, [node_dev] * chips + [node_dev * chips // 2] * 2, "backward"
    )
    late = swap(col_term[chips + 1], "row", 1)
    early = swap(col_term[chips], "row", 1)
    pair_sum = []
    for k in range(chips):
        start = (k % (chips // 2)) * node_dev
        got = (early, late)[k // (chips // 2)][start : start + node_dev]
        pair_sum.append(add(col_term[k], got))
    return (layer_out, add(*plane_reduce(pair_sum, "row", 4, 12, 2)))


def solution(mesh):
    in_specs = (
        P(("row", "col"), None),
        P(("row", "col")),
        P(),
        P(),
        P("row", "col", None),
        P("row", "col", None),
        P("row", "col"),
        P("row", "col", None, None, None),
        P("row", None),
    )
    out_specs = (P(("row", "col"), None), P(("col", "row"), None))
    return jax.shard_map(
        per_device, mesh=mesh, in_specs=in_specs, out_specs=out_specs, check_vma=False
    )
```
